256 devices in a mesh: band: 8 (over z), rows: 32 (over x, y, core).
Axes of the slice: x: 4, y: 4, z: 8, core: 2. Of those that a mesh axis runs over, the one named last changes fastest.
Arguments:
- tiles: bfloat16 [32, 8, 4, 512, 512], P('rows', 'band'), may hold values from -0.25 to 0.25
- tile_row: int32 [32, 8, 4], P('rows', 'band'), may hold values from 0 to 7
- tile_col: int32 [32, 8, 4], P('rows', 'band'), may hold values from 0 to 31
- tile_count: int32 [32, 8], P('rows', 'band'), may hold values from 1 to 4, as said below
- damping: float32 [128], replicated, may hold values from 0.5 to 2
- right_side: float32 [131072, 128], P(('rows', 'band')), may hold values from -40 to 40
Outputs:
- basis: float32 [4, 131072, 128], P(None, ('rows', 'band'))
- hessenberg: float32 [4, 3, 128], replicated
The draws below stay inside these ranges and needn't reach their ends.
Inputs may be any that keep to these rules, and one draw needn't show every extreme that they name: `tile_count`: slots at or past the count hold tiles that are not part of the matrix; some row shard and band holds exactly 4 live tiles.
All inputs are finite; a program needn't handle non-finite values.
Results may differ from the reference program's by a relative error of at most 0.007.
Values may be sent and summed in bfloat16 or wider, within the bound.
A program may use at most 64 MiB of HBM per device.

```python
import math
import jax
import jax.numpy as jnp
from jax import lax

TILE = 512
QUERIES = 128
TILES_DEV = 4
ITERS = 3
NDIM = 131072
N_BAND = 8
N_ROWS = 32


def draw_tile_count(key, part):
    first, second, third = jax.random.split(jax.random.fold_in(key, 17), 3)
    lower = jax.random.randint(first, (N_ROWS, N_BAND), 1, TILES_DEV + 1)
    upper = jax.random.randint(second, (N_ROWS, N_BAND), 1, TILES_DEV + 1)
    counts = jnp.minimum(lower, upper).reshape(-1)
    place = jax.random.randint(third, (), 0, N_ROWS * N_BAND)
    counts = counts.at[place].set(TILES_DEV)
    return counts.reshape(N_ROWS, N_BAND).astype(jnp.int32)


def draw_right_side(key, part):
    first = jax.random.fold_in(jax.random.fold_in(key, 29), 0)
    ramp = 1.0 + 2.0 * jnp.arange(NDIM, dtype=jnp.float32) / (NDIM - 1)
    values = jax.random.normal(first, (NDIM, QUERIES), jnp.float32) * ramp[:, None]
    return jnp.clip(values, -40.0, 40.0).astype(jnp.float32)


def plant(values, rng, least, largest):
    extent = values.shape
    index_at = [jax.random.randint(jax.random.fold_in(rng, axis), (), 0, extent[axis]) for axis in range(len(extent))]
    values = values.at[tuple(index_at)].set(least)
    longest = extent.index(max(extent))
    index_at[longest] = (index_at[longest] + 1) % extent[longest]
    return values.at[tuple(index_at)].set(largest)


def levels(own_key, shape, pieces, smallest, top_value):
    def one(position, blocks):
        draws = jax.random.uniform(jax.random.fold_in(jax.random.fold_in(own_key, 6), position), (blocks,), jnp.float32, smallest / len(pieces), top_value / len(pieces))
        return jnp.repeat(jnp.exp(draws), shape[position] // blocks).reshape((-1,) + (1,) * (len(shape) - position - 1))

    level = one(*pieces[0])
    for cut in pieces[1:]:
        level = level * one(*cut)
    return level


def normal_values(stream_key, shape, width, bound, shards=(), kind=jnp.bfloat16):
    loudness = levels(stream_key, shape, shards, -0.22, 0.18) if shards else 1.0
    drawn = jax.random.normal(stream_key, shape, jnp.float32) * width * loudness
    return jnp.minimum(jnp.maximum(drawn, -bound), bound).astype(kind)


def setup_inputs(seed: int = 0) -> dict:
    streams_of = jax.random.split(jax.random.key(seed), 7)
    return {
        "tiles": normal_values(streams_of[0], (N_ROWS, N_BAND, TILES_DEV, TILE, TILE), TILE ** -0.5, 0.25, ((0, 32), (1, 8))),
        "tile_row": plant(jax.random.randint(streams_of[1], (N_ROWS, N_BAND, TILES_DEV), 0, N_BAND), jax.random.fold_in(streams_of[1], 1), 0, N_BAND - 1).astype(jnp.int32),
        "tile_col": plant(jax.random.randint(streams_of[2], (N_ROWS, N_BAND, TILES_DEV), 0, N_ROWS), jax.random.fold_in(streams_of[2], 1), 0, N_ROWS - 1).astype(jnp.int32),
        "tile_count": draw_tile_count(jax.random.fold_in(streams_of[6], 71), 0),
        "damping": jnp.clip(jnp.exp(jax.random.uniform(streams_of[4], (QUERIES,), jnp.float32, math.log(0.5), math.log(2.0))), 0.5, 2.0),
        "right_side": draw_right_side(jax.random.fold_in(streams_of[6], 71), 0),
    }


EPS = 1e-06

def tile_product(tiles, tile_row, tile_col, tile_count, vector):
    columns = vector.astype(jnp.bfloat16).reshape(N_ROWS, N_BAND, TILE, QUERIES)
    slots = jnp.arange(TILES_DEV).astype(jnp.int32)
    targets = jnp.arange(N_BAND).astype(jnp.int32)

    def row_shard(shard):

        def add_band(running, band):
            band_columns = jnp.take(columns, band, axis=1)
            picked = jnp.take(band_columns, tile_col[shard, band], axis=0).astype(jnp.float32)
            local_tiles = tiles[shard, band].astype(jnp.float32)
            products = jnp.einsum('sij,sjq->siq', local_tiles, picked, precision=lax.Precision.HIGHEST)
            live = slots < tile_count[shard, band]
            onehot = ((tile_row[shard, band][:, None] == targets[None, :]) & live[:, None]).astype(jnp.float32)
            added = jnp.einsum('st,siq->tiq', onehot, products, precision=lax.Precision.HIGHEST)
            return (running + added, None)
        running, unused = lax.scan(add_band, jnp.zeros((N_BAND, TILE, QUERIES), jnp.float32), jnp.arange(N_BAND).astype(jnp.int32))
        return running
    return lax.map(row_shard, jnp.arange(N_ROWS).astype(jnp.int32)).reshape(NDIM, QUERIES)

def reference(tiles, tile_row, tile_col, tile_count, damping, right_side):
    start = lax.optimization_barrier(jnp.sum(right_side * right_side, axis=0))
    vectors = [right_side * lax.rsqrt(start + EPS)[None, :]]
    hessenberg = jnp.zeros((ITERS + 1, ITERS, QUERIES), jnp.float32)
    for step in range(ITERS):
        current = vectors[step]
        image = tile_product(tiles, tile_row, tile_col, tile_count, current) + damping[None, :] * current
        for other in range(step + 1):
            coefficient = lax.optimization_barrier(jnp.sum(vectors[other] * image, axis=0))
            image = image - coefficient[None, :] * vectors[other]
            hessenberg = hessenberg.at[other, step].set(coefficient)
        norm = jnp.sqrt(lax.optimization_barrier(jnp.sum(image * image, axis=0)) + EPS)
        hessenberg = hessenberg.at[step + 1, step].set(norm)
        vectors.append(image / norm[None, :])
    basis = jnp.stack(vectors) * math.sqrt(NDIM)
    return (basis, hessenberg)
```

```python
import functools
import math

import jax
import jax.numpy as jnp
from jax import lax
from jax.experimental import pallas as pl
from jax.experimental.pallas import tpu as pltpu
from jax.sharding import Mesh
from jax.sharding import PartitionSpec as P

EPS = 1e-06
ITERS = 3
SLOTS = 4
TILE = 512
QUERIES = 128
CHUNKS = 4
QC = QUERIES // CHUNKS
STAGGER = 2
NX, NY, NZ = 4, 4, 8
PLANE = NX * NY * 2


def wrap(value, count):
    return lax.rem(value + 2 * count, count)


def kernel(
    rescale,
    rows_ref, cols_ref, count_ref, damping_ref, right_ref, tiles_ref,
    basis_ref, hess_ref,
    *scratch,
):
    refs = list(scratch)
    gathered = [[refs.pop(0) for _ in range(CHUNKS)] for _ in range(ITERS)]
    sums_z = [[refs.pop(0) for _ in range(CHUNKS)] for _ in range(ITERS)]
    (tiles_in, tiles_t, right_v, vec, act, part, rs_send, damp_col, out_v, hess_v,
     ar_z, ar_x, ar_y, ar_c,
     in_sem, out_sem, ag_s, ag_r, rs_s, rs_r, ar_s, ar_r) = refs

    x, y, z, c = (lax.axis_index(name) for name in ("x", "y", "z", "c"))
    s = 1 - 2 * c

    tiles_copy = pltpu.make_async_copy(tiles_ref, tiles_in, in_sem.at[0])
    tiles_copy.start()
    right_copy = pltpu.make_async_copy(right_ref, right_v, in_sem.at[1])
    right_copy.start()

    barrier = pltpu.get_barrier_semaphore()
    peers = [{"z": wrap(z + k, NZ)} for k in range(1, NZ)]
    peers += [{"x": wrap(x + k, NX)} for k in range(1, NX)]
    peers += [{"y": wrap(y + k, NY)} for k in range(1, NY)]
    peers += [{"c": 1 - c}]
    for peer in peers:
        pl.semaphore_signal(barrier, inc=1, device_id=peer, device_id_type=pl.DeviceIdType.MESH)

    sent = []

    def send(src, dst, send_sem, recv_sem, peer):
        copy = pltpu.make_async_remote_copy(
            src_ref=src, dst_ref=dst, send_sem=send_sem, recv_sem=recv_sem,
            device_id=peer, device_id_type=pl.DeviceIdType.MESH,
        )
        copy.start()
        sent.append(copy)
        return copy

    right_copy.wait()
    for k in range(TILE // 128):
        vec[0, :, k * 128 : (k + 1) * 128] = right_v[k * 128 : (k + 1) * 128, :].T
    damp_row = damping_ref[...]
    lane = lax.broadcasted_iota(jnp.int32, (QC, 128), 1)
    sub = lax.broadcasted_iota(jnp.int32, (QC, 128), 0)
    hess_v[...] = jnp.zeros_like(hess_v)
    pl.semaphore_wait(barrier, len(peers))

    def setup():
        tiles_copy.wait()
        for slot in range(SLOTS):
            for k in range(TILE // 128):
                tiles_t[slot, :, k * 128 : (k + 1) * 128] = tiles_in[slot, k * 128 : (k + 1) * 128, :].T
            yield

    def chunk(ch):
        q0 = ch * QC
        qs = slice(q0, q0 + QC)
        eye = lane == sub + q0
        in_chunk = (lax.broadcasted_iota(jnp.int32, (1, 128), 1) // QC) == ch
        x_first = ch % 2 == 0
        first, second = ("x", "y") if x_first else ("y", "x")
        u, w = (x, y) if x_first else (y, x)

        def to_row(col):
            return jnp.sum(jnp.where(eye, col, 0.0), axis=0, keepdims=True)

        def to_col(row):
            return jnp.sum(jnp.where(eye, row, 0.0), axis=1, keepdims=True)

        def dot(a, b):
            return to_row(jnp.sum(a * b, axis=1, keepdims=True))

        def reduced(which, rows):
            result = []

            def run():
                filled = jnp.concatenate(
                    rows + [jnp.zeros((8 - len(rows), 128), jnp.float32)] * (len(rows) < 8), axis=0
                )
                stages = (("z", z, NZ, ar_z), ("x", x, NX, ar_x), ("y", y, NY, ar_y), ("c", c, 2, ar_c))
                total = filled
                for at, (axis, me, count, buf) in enumerate(stages):
                    here = buf.at[which, ch]
                    here[me] = total
                    copies = []
                    for k in range(1, count):
                        copies.append(send(
                            here.at[me], here.at[me], ar_s.at[which, ch, at, k - 1],
                            ar_r.at[which, ch, at, k - 1], {axis: wrap(me + k, count)},
                        ))
                    yield
                    for copy in copies:
                        copy.wait_recv()
                    total = here[0]
                    for k in range(1, count):
                        total = total + here[k]
                result.append(total)

            return run(), result

        gather = gathered[0][ch]
        own = c * 16 + w * 4 + u
        right = vec[0, qs, :]
        gather[own] = right.astype(jnp.bfloat16)
        summing, summed = reduced(0, [dot(right, right)])
        known = {}
        yield

        for step in range(ITERS):
            gather = gathered[step][ch]
            sem = lambda k: (ag_s.at[step, ch, k], ag_r.at[step, ch, k])
            row = lambda core, place: gather.at[pl.ds(core * 16 + place * 4, 4)]
            up = send(gather.at[own], gather.at[own], *sem(0), {first: wrap(u + s, 4)})
            down = send(gather.at[own], gather.at[own], *sem(1), {first: wrap(u - s, 4)})
            next(summing, None)
            yield
            up.wait_recv()
            behind = c * 16 + w * 4 + wrap(u - s, 4)
            relay = send(gather.at[behind], gather.at[behind], *sem(2), {first: wrap(u + s, 4)})
            next(summing, None)
            yield
            down.wait_recv()
            relay.wait_recv()
            mine = row(c, w)
            up = send(mine, mine, *sem(3), {second: wrap(w + s, 4)})
            down = send(mine, mine, *sem(4), {second: wrap(w - s, 4)})
            twin = [send(mine, mine, *sem(6), {"c": 1 - c})]
            next(summing, None)
            yield
            up.wait_recv()
            behind = row(c, wrap(w - s, 4))
            relay = send(behind, behind, *sem(5), {second: wrap(w + s, 4)})
            twin.append(send(behind, behind, *sem(7), {"c": 1 - c}))
            down.wait_recv()
            ahead = row(c, wrap(w + s, 4))
            twin.append(send(ahead, ahead, *sem(8), {"c": 1 - c}))
            next(summing, None)
            yield
            relay.wait_recv()
            across = row(c, wrap(w + 2, 4))
            twin.append(send(across, across, *sem(9), {"c": 1 - c}))
            next(summing, None)
            yield
            for copy in twin:
                copy.wait_recv()
            products = []
            for slot in range(SLOTS):
                col = cols_ref[slot]
                cx, cy, cc = col // 8, lax.rem(col // 2, 4), lax.rem(col, 2)
                place = cc * 16 + (cy * 4 + cx if x_first else cx * 4 + cy)
                products.append(jnp.dot(
                    gather[place], tiles_t[slot], preferred_element_type=jnp.float32
                ))
            for target in range(NZ):
                total = None
                for slot in range(SLOTS):
                    live = jnp.logical_and(rows_ref[slot] == target, slot < count_ref[0])
                    term = products[slot] * jnp.where(live, 1.0, 0.0)
                    total = term if total is None else total + term
                part[ch, target] = total

            arrive = sums_z[step][ch]

            def pass_on(k, value, direction):
                out = rs_send.at[step, ch, k]
                out[...] = value.astype(jnp.bfloat16)
                return send(
                    out, arrive.at[k], rs_s.at[step, ch, k], rs_r.at[step, ch, k],
                    {"z": wrap(z + direction, NZ)},
                )

            def mine_for(k):
                return part[ch, wrap(z + k * s, NZ)]

            fore = pass_on(0, mine_for(4), s)
            back = pass_on(4, mine_for(-3), -s)
            yield
            for k in range(1, 4):
                fore.wait_recv()
                fore = pass_on(k, mine_for(4 - k) + arrive[k - 1].astype(jnp.float32), s)
                if k < 3:
                    back.wait_recv()
                    back = pass_on(4 + k, mine_for(k - 3) + arrive[3 + k].astype(jnp.float32), -s)
                yield
            back.wait_recv()
            raw = part[ch, z] + arrive[6].astype(jnp.float32)
            fore.wait_recv()
            raw = raw + arrive[3].astype(jnp.float32)

            for _ in summing:
                pass
            g = summed[0]
            d = damp_row
            if step == 0:
                known["inv"] = lax.rsqrt(g[0:1] + EPS)
                inv = to_col(known["inv"])
                image = raw * inv
                v0 = vec[0, qs, :] * inv
                vec[0, qs, :] = v0
                act[0, qs, :] = image
                dots = [dot(v0, image), dot(image, image), dot(v0, v0)]
            elif step == 1:
                va, aa, vv = g[0:1], g[1:2], g[2:3]
                h00 = va + d * vv
                e = d - h00
                square = aa + 2.0 * e * va + e * e * vv
                h10 = jnp.sqrt(jnp.maximum(square, 0.0) + EPS)
                known.update(vv00=vv)
                store(0, 0, h00, in_chunk)
                store(1, 0, h10, in_chunk)
                e_col, h_col = to_col(e), to_col(1.0 / h10)
                v0, a0 = vec[0, qs, :], act[0, qs, :]
                v1 = (a0 + e_col * v0) * h_col
                image = (raw + e_col * a0) * h_col
                vec[1, qs, :] = v1
                act[1, qs, :] = image
                dots = [dot(v0, image), dot(v1, image), dot(image, image), dot(v0, v1), dot(v1, v1)]
            else:
                va0, va1, aa, v01, v11 = (g[k : k + 1] for k in range(5))
                v00 = known["vv00"]
                h01 = va0 + d * v01
                h11 = va1 + d * v11 - h01 * v01
                e = d - h11
                square = (
                    aa + e * e * v11 + h01 * h01 * v00
                    + 2.0 * e * va1 - 2.0 * h01 * va0 - 2.0 * e * h01 * v01
                )
                h21 = jnp.sqrt(jnp.maximum(square, 0.0) + EPS)
                known.update(v01=v01, v11=v11)
                store(0, 1, h01, in_chunk)
                store(1, 1, h11, in_chunk)
                store(2, 1, h21, in_chunk)
                e_col, f_col, h_col = to_col(e), to_col(h01), to_col(1.0 / h21)
                v0, v1 = vec[0, qs, :], vec[1, qs, :]
                a0, a1 = act[0, qs, :], act[1, qs, :]
                v2 = (a1 + e_col * v1 - f_col * v0) * h_col
                image = (raw + e_col * a1 - f_col * a0) * h_col
                vec[2, qs, :] = v2
                dots = [
                    dot(v0, image), dot(v1, image), dot(v2, image), dot(image, image),
                    dot(v0, v2), dot(v1, v2), dot(v2, v2),
                ]
            if step + 1 < ITERS:
                gathered[step + 1][ch][own] = image.astype(jnp.bfloat16)
            summing, summed = reduced(step + 1, dots)
            if step + 1 == ITERS:
                next(summing)
                yield
                for _ in summing:
                    yield

        va0, va1, va2, aa, v02, v12, v22 = (summed[0][k : k + 1] for k in range(7))
        v00, v01, v11 = known["vv00"], known["v01"], known["v11"]
        d = damp_row
        h02 = va0 + d * v02
        h12 = va1 + d * v12 - h02 * v01
        h22 = va2 + d * v22 - h02 * v02 - h12 * v12
        e = d - h22
        square = (
            aa + e * e * v22 + h02 * h02 * v00 + h12 * h12 * v11
            + 2.0 * (e * va2 - h02 * va0 - h12 * va1 - e * h02 * v02 - e * h12 * v12 + h02 * h12 * v01)
        )
        h32 = jnp.sqrt(jnp.maximum(square, 0.0) + EPS)
        store(0, 2, h02, in_chunk)
        store(1, 2, h12, in_chunk)
        store(2, 2, h22, in_chunk)
        store(3, 2, h32, in_chunk)
        e_col, f_col, k_col, h_col = to_col(e), to_col(h02), to_col(h12), to_col(1.0 / h32)
        vec[3, qs, :] = (image + e_col * vec[2, qs, :] - f_col * vec[0, qs, :] - k_col * vec[1, qs, :]) * h_col

    def store(i, j, row, mask):
        at = i * ITERS + j
        hess_v[at : at + 1, :] = jnp.where(mask, row, hess_v[at : at + 1, :])

    outs = []

    def emit(i):
        for k in range(TILE // 128):
            out_v[i, k * 128 : (k + 1) * 128, :] = vec[i, :, k * 128 : (k + 1) * 128].T * rescale
        copy = pltpu.make_async_copy(out_v.at[i], basis_ref.at[i], out_sem.at[i])
        copy.start()
        outs.append(copy)

    live = {ch: chunk(ch) for ch in range(CHUNKS)}
    preparing = setup()
    tick = 0
    ticks = {ch: 0 for ch in range(CHUNKS)}
    emitted = 0
    while live:
        for ch in list(live):
            if tick >= ch * STAGGER:
                try:
                    next(live[ch])
                    ticks[ch] += 1
                except StopIteration:
                    del live[ch]
        next(preparing, None)
        tick += 1
        if emitted < ITERS and min(ticks.values()) > 1 + 9 * (emitted + 1):
            emit(emitted)
            emitted += 1
    while emitted < ITERS + 1:
        emit(emitted)
        emitted += 1
    hess_copy = pltpu.make_async_copy(hess_v, hess_ref, out_sem.at[ITERS + 1])
    hess_copy.start()
    for copy in sent:
        copy.wait_send()
    for copy in outs:
        copy.wait()
    hess_copy.wait()


def on_device(tiles, tile_row, tile_col, tile_count, damping, right_side):
    width, queries = right_side.shape
    rescale = math.sqrt(width * NX * NY * NZ * 2)
    smem = pl.BlockSpec(memory_space=pltpu.SMEM)
    vmem = pl.BlockSpec(memory_space=pltpu.VMEM)
    hbm = pl.BlockSpec(memory_space=pl.ANY)
    dma = pltpu.SemaphoreType.DMA
    bf16, f32 = jnp.bfloat16, jnp.float32
    basis, hessenberg = pl.pallas_call(
        functools.partial(kernel, rescale),
        out_shape=(
            jax.ShapeDtypeStruct((ITERS + 1, width, queries), f32),
            jax.ShapeDtypeStruct(((ITERS + 1) * ITERS, queries), f32),
        ),
        in_specs=[smem, smem, smem, vmem, hbm, hbm],
        out_specs=(hbm, hbm),
        scratch_shapes=[pltpu.VMEM((PLANE, QC, TILE), bf16) for _ in range(ITERS * CHUNKS)]
        + [pltpu.VMEM((7, QC, TILE), bf16) for _ in range(ITERS * CHUNKS)]
        + [
            pltpu.VMEM((SLOTS, TILE, TILE), bf16),
            pltpu.VMEM((SLOTS, TILE, TILE), bf16),
            pltpu.VMEM((TILE, QUERIES), f32),
            pltpu.VMEM((ITERS + 1, QUERIES, TILE), f32),
            pltpu.VMEM((ITERS, QUERIES, TILE), f32),
            pltpu.VMEM((CHUNKS, NZ, QC, TILE), f32),
            pltpu.VMEM((ITERS, CHUNKS, 7, QC, TILE), bf16),
            pltpu.VMEM((8, QUERIES), f32),
            pltpu.VMEM((ITERS + 1, TILE, QUERIES), f32),
            pltpu.VMEM(((ITERS + 1) * ITERS, QUERIES), f32),
            pltpu.VMEM((ITERS + 1, CHUNKS, NZ, 8, 128), f32),
            pltpu.VMEM((ITERS + 1, CHUNKS, NX, 8, 128), f32),
            pltpu.VMEM((ITERS + 1, CHUNKS, NY, 8, 128), f32),
            pltpu.VMEM((ITERS + 1, CHUNKS, 2, 8, 128), f32),
            dma((2,)),
            dma((ITERS + 2,)),
            dma((ITERS, CHUNKS, 10)),
            dma((ITERS, CHUNKS, 10)),
            dma((ITERS, CHUNKS, 7)),
            dma((ITERS, CHUNKS, 7)),
            dma((ITERS + 1, CHUNKS, 4, 7)),
            dma((ITERS + 1, CHUNKS, 4, 7)),
        ],
        compiler_params=pltpu.CompilerParams(
            collective_id=0, has_side_effects=True, vmem_limit_bytes=60 * 1024 * 1024
        ),
    )(
        tile_row.reshape(SLOTS), tile_col.reshape(SLOTS), tile_count.reshape(1),
        damping.reshape(1, queries), right_side, tiles.reshape(SLOTS, TILE, TILE),
    )
    return basis, hessenberg.reshape(ITERS + 1, ITERS, queries)


def solution(mesh):
    finer = Mesh(mesh.devices.reshape(NZ, NX, NY, 2), ("z", "x", "y", "c"))
    rows = ("x", "y", "c")
    return jax.shard_map(
        on_device,
        mesh=finer,
        in_specs=(
            P(rows, "z", None, None, None),
            P(rows, "z", None),
            P(rows, "z", None),
            P(rows, "z"),
            P(),
            P((*rows, "z"), None),
        ),
        out_specs=(P(None, (*rows, "z"), None), P()),
        check_vma=False,
    )
```

```python
import functools
import math

import jax
import jax.numpy as jnp
from jax import lax
from jax.experimental import pallas as pl
from jax.experimental.pallas import tpu as pltpu
from jax.sharding import Mesh
from jax.sharding import PartitionSpec as P

EPS = 1e-06
ITERS = 3
SLOTS = 4
TILE = 512
QUERIES = 128
CHUNKS = 4
QC = QUERIES // CHUNKS
GROUP = 4
STAGGER = 0
STEP_TICKS = 8
SUM_TICKS = (1, 2, 5)
NX, NY, NZ = 4, 4, 8
PLANE = NX * NY * 2


def wrap(value, count):
    return lax.rem(value + 2 * count, count)


def kernel(
    rescale,
    rows_ref, cols_ref, count_ref, damping_ref, right_ref, tiles_ref,
    basis_ref, hess_ref,
    *scratch,
):
    refs = list(scratch)
    gathered = [[refs.pop(0) for _ in range(CHUNKS)] for _ in range(ITERS)]
    sums_z = [[refs.pop(0) for _ in range(CHUNKS)] for _ in range(ITERS)]
    (tiles_in, tiles_t, right_v, vec, act, part, rs_send, damp_col, out_v, hess_v,
     ar_z, ar_xy, ar_c,
     in_sem, out_sem, ag_s, ag_r, rs_s, rs_r, ar_s, ar_r) = refs

    x, y, z, c = (lax.axis_index(name) for name in ("x", "y", "z", "c"))
    s = 1 - 2 * c

    tiles_copy = pltpu.make_async_copy(tiles_ref, tiles_in, in_sem.at[0])
    tiles_copy.start()
    right_copy = pltpu.make_async_copy(right_ref, right_v, in_sem.at[1])
    right_copy.start()

    barrier = pltpu.get_barrier_semaphore()
    across_z = [{"z": wrap(z + k, NZ)} for k in range(1, NZ)]
    across_xy = [
        {"x": wrap(x + i, NX), "y": wrap(y + k, NY)}
        for i, k in ((2, 2), (1, 2), (3, 2), (2, 1), (2, 3), (1, 1), (3, 3), (1, 3), (3, 1),
                     (2, 0), (0, 2), (1, 0), (3, 0), (0, 1), (0, 3))
    ]
    peers = across_z + across_xy + [{"c": 1 - c}]
    for peer in peers:
        pl.semaphore_signal(barrier, inc=1, device_id=peer, device_id_type=pl.DeviceIdType.MESH)

    sent = []

    def remote(src, dst, send_sem, recv_sem, peer):
        return pltpu.make_async_remote_copy(
            src_ref=src, dst_ref=dst, send_sem=send_sem, recv_sem=recv_sem,
            device_id=peer, device_id_type=pl.DeviceIdType.MESH,
        )

    def send(*what):
        remote(*what).start()

    def send_one(*what):
        copy = remote(*what)
        copy.start()
        sent.append(copy)
        return copy

    def await_recv(size, send_sem, recv_sem):
        remote(size, size, send_sem, recv_sem, {"c": 1 - c}).wait_recv()

    def await_send(size, send_sem, recv_sem):
        sent.append(remote(size, size, send_sem, recv_sem, {"c": 1 - c}))

    right_copy.wait()
    for k in range(TILE // 128):
        vec[0, :, k * 128 : (k + 1) * 128] = right_v[k * 128 : (k + 1) * 128, :].T
    damp_row = damping_ref[...]
    lane = lax.broadcasted_iota(jnp.int32, (QC, 128), 1)
    sub = lax.broadcasted_iota(jnp.int32, (QC, 128), 0)
    hess_v[...] = jnp.zeros_like(hess_v)
    pl.semaphore_wait(barrier, len(peers))

    def setup():
        tiles_copy.wait()
        for slot in range(SLOTS):
            for k in range(TILE // 128):
                tiles_t[slot, :, k * 128 : (k + 1) * 128] = tiles_in[slot, k * 128 : (k + 1) * 128, :].T
            yield

    def reduced(which, group, rows):
        result = []

        def run():
            pad = [jnp.zeros((8 - len(rows), 128), jnp.float32)] if len(rows) < 8 else []
            total = jnp.concatenate(rows + pad, axis=0)
            stages = (
                (c, [{"c": 1 - c}], ar_c), (z, across_z, ar_z), (x * NY + y, across_xy, ar_xy)
            )
            for at, (me, others, buf) in enumerate(stages):
                here = buf.at[which, group]
                here[me] = total
                sems = ar_s.at[which, group, at], ar_r.at[which, group, at]
                for peer in others:
                    send(here.at[me], here.at[me], *sems, peer)
                await_send(here.at[pl.ds(0, len(others))], *sems)
                yield
                await_recv(here.at[pl.ds(0, len(others))], *sems)
                total = here[0]
                for k in range(1, len(others) + 1):
                    total = total + here[k]
            result.append(total)

        return run(), result

    def chunk(ch, shared):
        q0 = ch * QC
        qs = slice(q0, q0 + QC)
        eye = lane == sub + q0
        in_chunk = (lax.broadcasted_iota(jnp.int32, (1, 128), 1) // QC) == ch
        x_first = ch % 2 == 0
        first, second = ("x", "y") if x_first else ("y", "x")
        u, w = (x, y) if x_first else (y, x)

        def to_row(col):
            return jnp.sum(jnp.where(eye, col, 0.0), axis=0, keepdims=True)

        def to_col(row):
            return jnp.sum(jnp.where(eye, row, 0.0), axis=1, keepdims=True)

        def dot(a, b):
            return to_row(jnp.sum(a * b, axis=1, keepdims=True))

        gather = gathered[0][ch]
        own = c * 16 + w * 4 + u
        right = vec[0, qs, :]
        gather[own] = right.astype(jnp.bfloat16)
        shared["rows"].append([dot(right, right)])
        known = {}

        def row(core, place):
            return gather.at[pl.ds(core * 16 + place * 4, 4)]

        def pair(step, k):
            return ag_s.at[step, ch, k], ag_r.at[step, ch, k]

        for step in range(ITERS):
            gather = gathered[step][ch]
            early = pair(step, 0)
            for k in (2, 1, 3):
                send(gather.at[own], gather.at[own], *early, {first: wrap(u + k, 4)})
            await_send(gather.at[pl.ds(0, 3)], *early)
            yield
            await_recv(gather.at[pl.ds(0, 3)], *early)
            mine = row(c, w)
            up = send_one(mine, mine, *pair(step, 1), {second: wrap(w + s, 4)})
            down = send_one(mine, mine, *pair(step, 2), {second: wrap(w - s, 4)})
            twin = pair(step, 4)
            send(mine, mine, *twin, {"c": 1 - c})
            yield
            up.wait_recv()
            behind = row(c, wrap(w - s, 4))
            relay = send_one(behind, behind, *pair(step, 3), {second: wrap(w + s, 4)})
            send(behind, behind, *twin, {"c": 1 - c})
            down.wait_recv()
            ahead = row(c, wrap(w + s, 4))
            send(ahead, ahead, *twin, {"c": 1 - c})
            yield
            relay.wait_recv()
            opposite = row(c, wrap(w + 2, 4))
            send(opposite, opposite, *twin, {"c": 1 - c})
            await_send(gather.at[pl.ds(0, 16)], *twin)
            yield
            await_recv(gather.at[pl.ds(0, 16)], *twin)
            products = []
            for slot in range(SLOTS):
                col = cols_ref[slot]
                cx, cy, cc = col // 8, lax.rem(col // 2, 4), lax.rem(col, 2)
                place = cc * 16 + (cy * 4 + cx if x_first else cx * 4 + cy)
                products.append(jnp.dot(
                    gather[place], tiles_t[slot], preferred_element_type=jnp.float32
                ))
            for target in range(NZ):
                total = None
                for slot in range(SLOTS):
                    live = jnp.logical_and(rows_ref[slot] == target, slot < count_ref[0])
                    term = products[slot] * jnp.where(live, 1.0, 0.0)
                    total = term if total is None else total + term
                part[ch, target] = total

            arrive = sums_z[step][ch]

            def pass_on(k, value, direction):
                out = rs_send.at[step, ch, k]
                out[...] = value.astype(jnp.bfloat16)
                return send_one(
                    out, arrive.at[k], rs_s.at[step, ch, k], rs_r.at[step, ch, k],
                    {"z": wrap(z + direction, NZ)},
                )

            def mine_for(k):
                return part[ch, wrap(z + k * s, NZ)]

            fore = pass_on(0, mine_for(4), s)
            back = pass_on(4, mine_for(-3), -s)
            yield
            for k in range(1, 4):
                fore.wait_recv()
                fore = pass_on(k, mine_for(4 - k) + arrive[k - 1].astype(jnp.float32), s)
                if k < 3:
                    back.wait_recv()
                    back = pass_on(4 + k, mine_for(k - 3) + arrive[3 + k].astype(jnp.float32), -s)
                yield
            back.wait_recv()
            raw = part[ch, z] + arrive[6].astype(jnp.float32)
            fore.wait_recv()
            raw = raw + arrive[3].astype(jnp.float32)

            g = shared["total"]
            d = damp_row
            if step == 0:
                known["inv"] = lax.rsqrt(g[0:1] + EPS)
                inv = to_col(known["inv"])
                image = raw * inv
                v0 = vec[0, qs, :] * inv
                vec[0, qs, :] = v0
                act[0, qs, :] = image
                dots = [dot(v0, image), dot(image, image), dot(v0, v0)]
            elif step == 1:
                va, aa, vv = g[0:1], g[1:2], g[2:3]
                h00 = va + d * vv
                e = d - h00
                square = aa + 2.0 * e * va + e * e * vv
                h10 = jnp.sqrt(jnp.maximum(square, 0.0) + EPS)
                known.update(vv00=vv)
                store(0, 0, h00, in_chunk)
                store(1, 0, h10, in_chunk)
                e_col, h_col = to_col(e), to_col(1.0 / h10)
                v0, a0 = vec[0, qs, :], act[0, qs, :]
                v1 = (a0 + e_col * v0) * h_col
                image = (raw + e_col * a0) * h_col
                vec[1, qs, :] = v1
                act[1, qs, :] = image
                dots = [dot(v0, image), dot(v1, image), dot(image, image), dot(v0, v1), dot(v1, v1)]
            else:
                va0, va1, aa, v01, v11 = (g[k : k + 1] for k in range(5))
                v00 = known["vv00"]
                h01 = va0 + d * v01
                h11 = va1 + d * v11 - h01 * v01
                e = d - h11
                square = (
                    aa + e * e * v11 + h01 * h01 * v00
                    + 2.0 * e * va1 - 2.0 * h01 * va0 - 2.0 * e * h01 * v01
                )
                h21 = jnp.sqrt(jnp.maximum(square, 0.0) + EPS)
                known.update(v01=v01, v11=v11)
                store(0, 1, h01, in_chunk)
                store(1, 1, h11, in_chunk)
                store(2, 1, h21, in_chunk)
                e_col, f_col, h_col = to_col(e), to_col(h01), to_col(1.0 / h21)
                v0, v1 = vec[0, qs, :], vec[1, qs, :]
                a0, a1 = act[0, qs, :], act[1, qs, :]
                v2 = (a1 + e_col * v1 - f_col * v0) * h_col
                image = (raw + e_col * a1 - f_col * a0) * h_col
                vec[2, qs, :] = v2
                dots = [
                    dot(v0, image), dot(v1, image), dot(v2, image), dot(image, image),
                    dot(v0, v2), dot(v1, v2), dot(v2, v2),
                ]
            if step + 1 < ITERS:
                gathered[step + 1][ch][own] = image.astype(jnp.bfloat16)
            shared["rows"].append(dots)
        yield

        g = shared["total"]
        va0, va1, va2, aa, v02, v12, v22 = (g[k : k + 1] for k in range(7))
        v00, v01, v11 = known["vv00"], known["v01"], known["v11"]
        d = damp_row
        h02 = va0 + d * v02
        h12 = va1 + d * v12 - h02 * v01
        h22 = va2 + d * v22 - h02 * v02 - h12 * v12
        e = d - h22
        square = (
            aa + e * e * v22 + h02 * h02 * v00 + h12 * h12 * v11
            + 2.0 * (e * va2 - h02 * va0 - h12 * va1 - e * h02 * v02 - e * h12 * v12 + h02 * h12 * v01)
        )
        h32 = jnp.sqrt(jnp.maximum(square, 0.0) + EPS)
        store(0, 2, h02, in_chunk)
        store(1, 2, h12, in_chunk)
        store(2, 2, h22, in_chunk)
        store(3, 2, h32, in_chunk)
        e_col, f_col, k_col, h_col = to_col(e), to_col(h02), to_col(h12), to_col(1.0 / h32)
        vec[3, qs, :] = (image + e_col * vec[2, qs, :] - f_col * vec[0, qs, :] - k_col * vec[1, qs, :]) * h_col

    def store(i, j, row, mask):
        hess_v[i, j : j + 1, :] = jnp.where(mask, row, hess_v[i, j : j + 1, :])

    outs = []

    def emit(i):
        for k in range(TILE // 128):
            out_v[i, k * 128 : (k + 1) * 128, :] = vec[i, :, k * 128 : (k + 1) * 128].T * rescale
        copy = pltpu.make_async_copy(out_v.at[i], basis_ref.at[i], out_sem.at[i])
        copy.start()
        outs.append(copy)

    def together(group):
        shared = {"rows": [], "total": None}
        members = [chunk(group * GROUP + k, shared) for k in range(GROUP)]
        for which in range(ITERS + 1):
            for member in members:
                next(member)
            rows = [functools.reduce(jnp.add, same) for same in zip(*shared["rows"])]
            shared["rows"] = []
            summing, result = reduced(which, group, rows)
            next(summing)
            yield
            if which < ITERS:
                for tick in range(1, STEP_TICKS):
                    if tick in SUM_TICKS:
                        next(summing, None)
                    for member in members:
                        next(member)
                    yield
            for _ in summing:
                if which == ITERS:
                    yield
            shared["total"] = result[0]
        for member in members:
            next(member, None)

    groups = CHUNKS // GROUP
    live = {group: together(group) for group in range(groups)}
    ticks = [0] * groups
    tick = 0
    emitted = 0
    while live:
        for group in list(live):
            if tick >= group * STAGGER:
                try:
                    next(live[group])
                    ticks[group] += 1
                except StopIteration:
                    del live[group]
        if tick == 0:
            for _ in setup():
                pass
        tick += 1
        if emitted < ITERS and min(ticks) > STEP_TICKS * (emitted + 1):
            emit(emitted)
            emitted += 1
    while emitted < ITERS + 1:
        emit(emitted)
        emitted += 1
    hess_copy = pltpu.make_async_copy(hess_v, hess_ref, out_sem.at[ITERS + 1])
    hess_copy.start()
    for copy in sent:
        copy.wait_send()
    for copy in outs:
        copy.wait()
    hess_copy.wait()


def on_device(tiles, tile_row, tile_col, tile_count, damping, right_side):
    width, queries = right_side.shape
    rescale = math.sqrt(width * NX * NY * NZ * 2)
    smem = pl.BlockSpec(memory_space=pltpu.SMEM)
    vmem = pl.BlockSpec(memory_space=pltpu.VMEM)
    hbm = pl.BlockSpec(memory_space=pl.ANY)
    dma = pltpu.SemaphoreType.DMA
    bf16, f32 = jnp.bfloat16, jnp.float32
    basis, hessenberg = pl.pallas_call(
        functools.partial(kernel, rescale),
        out_shape=(
            jax.ShapeDtypeStruct((ITERS + 1, width, queries), f32),
            jax.ShapeDtypeStruct((ITERS + 1, ITERS, queries), f32),
        ),
        in_specs=[smem, smem, smem, vmem, hbm, hbm],
        out_specs=(hbm, hbm),
        scratch_shapes=[pltpu.VMEM((PLANE, QC, TILE), bf16) for _ in range(ITERS * CHUNKS)]
        + [pltpu.VMEM((7, QC, TILE), bf16) for _ in range(ITERS * CHUNKS)]
        + [
            pltpu.VMEM((SLOTS, TILE, TILE), bf16),
            pltpu.VMEM((SLOTS, TILE, TILE), bf16),
            pltpu.VMEM((TILE, QUERIES), f32),
            pltpu.VMEM((ITERS + 1, QUERIES, TILE), f32),
            pltpu.VMEM((ITERS, QUERIES, TILE), f32),
            pltpu.VMEM((CHUNKS, NZ, QC, TILE), f32),
            pltpu.VMEM((ITERS, CHUNKS, 7, QC, TILE), bf16),
            pltpu.VMEM((8, QUERIES), f32),
            pltpu.VMEM((ITERS + 1, TILE, QUERIES), f32),
            pltpu.VMEM((ITERS + 1, ITERS, QUERIES), f32),
            pltpu.VMEM((ITERS + 1, CHUNKS // GROUP, NZ, 8, 128), f32),
            pltpu.VMEM((ITERS + 1, CHUNKS // GROUP, NX * NY, 8, 128), f32),
            pltpu.VMEM((ITERS + 1, CHUNKS // GROUP, 2, 8, 128), f32),
            dma((2,)),
            dma((ITERS + 2,)),
            dma((ITERS, CHUNKS, 5)),
            dma((ITERS, CHUNKS, 5)),
            dma((ITERS, CHUNKS, 7)),
            dma((ITERS, CHUNKS, 7)),
            dma((ITERS + 1, CHUNKS // GROUP, 3)),
            dma((ITERS + 1, CHUNKS // GROUP, 3)),
        ],
        compiler_params=pltpu.CompilerParams(
            collective_id=0, has_side_effects=True, vmem_limit_bytes=60 * 1024 * 1024
        ),
    )(
        tile_row.reshape(SLOTS), tile_col.reshape(SLOTS), tile_count.reshape(1),
        damping.reshape(1, queries), right_side, tiles.reshape(SLOTS, TILE, TILE),
    )
    return basis, hessenberg


def solution(mesh):
    finer = Mesh(mesh.devices.reshape(NZ, NX, NY, 2), ("z", "x", "y", "c"))
    rows = ("x", "y", "c")
    return jax.shard_map(
        on_device,
        mesh=finer,
        in_specs=(
            P(rows, "z", None, None, None),
            P(rows, "z", None),
            P(rows, "z", None),
            P(rows, "z"),
            P(),
            P((*rows, "z"), None),
        ),
        out_specs=(P(None, (*rows, "z"), None), P()),
        check_vma=False,
    )
```

```python
import functools
import math

import jax
import jax.numpy as jnp
from jax import lax
from jax.experimental import pallas as pl
from jax.experimental.pallas import tpu as pltpu
from jax.sharding import Mesh
from jax.sharding import PartitionSpec as P

EPS = 1e-06
ITERS = 3
SLOTS = 4
TILE = 512
QUERIES = 128
CHUNKS = 4
QC = QUERIES // CHUNKS
GROUP = 4
STAGGER = 0
STEP_TICKS = 8
SUM_TICKS = (2,)
NX, NY, NZ = 4, 4, 8
PLANE = NX * NY * 2


def wrap(value, count):
    return lax.rem(value + 2 * count, count)


def kernel(
    rescale,
    rows_ref, cols_ref, count_ref, damping_ref, right_ref, tiles_ref,
    basis_ref, hess_ref,
    *scratch,
):
    refs = list(scratch)
    gathered = [[refs.pop(0) for _ in range(CHUNKS)] for _ in range(ITERS)]
    sums_z = [[refs.pop(0) for _ in range(CHUNKS)] for _ in range(ITERS)]
    (tiles_in, tiles_t, right_v, vec, act, part, rs_send, damp_col, out_v, hess_v,
     ar_zc, ar_xy,
     in_sem, out_sem, ag_s, ag_r, rs_s, rs_r, ar_s, ar_r) = refs

    x, y, z, c = (lax.axis_index(name) for name in ("x", "y", "z", "c"))
    s = 1 - 2 * c

    tiles_copy = pltpu.make_async_copy(tiles_ref, tiles_in, in_sem.at[0])
    tiles_copy.start()
    right_copy = pltpu.make_async_copy(right_ref, right_v, in_sem.at[1])
    right_copy.start()

    barrier = pltpu.get_barrier_semaphore()
    across_zc = [
        {"z": wrap(z + k, NZ), "c": core} for k in (4, 3, 5, 2, 6, 1, 7) for core in (1 - c, c)
    ] + [{"c": 1 - c}]
    across_xy = [
        {"x": wrap(x + i, NX), "y": wrap(y + k, NY)}
        for i, k in ((2, 2), (1, 2), (3, 2), (2, 1), (2, 3), (1, 1), (3, 3), (1, 3), (3, 1),
                     (2, 0), (0, 2), (1, 0), (3, 0), (0, 1), (0, 3))
    ]
    peers = across_zc + across_xy
    for peer in peers:
        pl.semaphore_signal(barrier, inc=1, device_id=peer, device_id_type=pl.DeviceIdType.MESH)

    sent = []

    def remote(src, dst, send_sem, recv_sem, peer):
        return pltpu.make_async_remote_copy(
            src_ref=src, dst_ref=dst, send_sem=send_sem, recv_sem=recv_sem,
            device_id=peer, device_id_type=pl.DeviceIdType.MESH,
        )

    def send(*what):
        remote(*what).start()

    def send_one(*what):
        copy = remote(*what)
        copy.start()
        sent.append(copy)
        return copy

    def await_recv(size, send_sem, recv_sem):
        remote(size, size, send_sem, recv_sem, {"c": 1 - c}).wait_recv()

    def await_send(size, send_sem, recv_sem):
        sent.append(remote(size, size, send_sem, recv_sem, {"c": 1 - c}))

    right_copy.wait()
    for k in range(TILE // 128):
        vec[0, :, k * 128 : (k + 1) * 128] = right_v[k * 128 : (k + 1) * 128, :].T
    damp_row = damping_ref[...]
    lane = lax.broadcasted_iota(jnp.int32, (QC, 128), 1)
    sub = lax.broadcasted_iota(jnp.int32, (QC, 128), 0)
    hess_v[...] = jnp.zeros_like(hess_v)
    pl.semaphore_wait(barrier, len(peers))

    def setup():
        tiles_copy.wait()
        for slot in range(SLOTS):
            for k in range(TILE // 128):
                tiles_t[slot, :, k * 128 : (k + 1) * 128] = tiles_in[slot, k * 128 : (k + 1) * 128, :].T
            yield

    def reduced(which, group, rows):
        result = []

        def run():
            pad = [jnp.zeros((8 - len(rows), 128), jnp.float32)] if len(rows) < 8 else []
            total = jnp.concatenate(rows + pad, axis=0)
            stages = ((z * 2 + c, across_zc, ar_zc), (x * NY + y, across_xy, ar_xy))
            for at, (me, others, buf) in enumerate(stages):
                here = buf.at[which, group]
                here[me] = total
                sems = ar_s.at[which, group, at], ar_r.at[which, group, at]
                for peer in others:
                    send(here.at[me], here.at[me], *sems, peer)
                await_send(here.at[pl.ds(0, len(others))], *sems)
                yield
                await_recv(here.at[pl.ds(0, len(others))], *sems)
                total = here[0]
                for k in range(1, len(others) + 1):
                    total = total + here[k]
            result.append(total)

        return run(), result

    def chunk(ch, shared):
        q0 = ch * QC
        qs = slice(q0, q0 + QC)
        eye = lane == sub + q0
        in_chunk = (lax.broadcasted_iota(jnp.int32, (1, 128), 1) // QC) == ch
        x_first = ch % 2 == 0
        first, second = ("x", "y") if x_first else ("y", "x")
        u, w = (x, y) if x_first else (y, x)

        def to_row(col):
            return jnp.sum(jnp.where(eye, col, 0.0), axis=0, keepdims=True)

        def to_col(row):
            return jnp.sum(jnp.where(eye, row, 0.0), axis=1, keepdims=True)

        def dot(a, b):
            return to_row(jnp.sum(a * b, axis=1, keepdims=True))

        gather = gathered[0][ch]
        own = c * 16 + w * 4
        right = vec[0, qs, :]
        gather[own] = right.astype(jnp.bfloat16)
        shared["rows"].append([dot(right, right)])
        known = {}

        def row(core, place):
            return gather.at[pl.ds(core * 16 + place * 4, 4)]

        def pair(step, k):
            return ag_s.at[step, ch, k], ag_r.at[step, ch, k]

        for step in range(ITERS):
            gather = gathered[step][ch]
            early, twin = pair(step, 0), pair(step, 4)
            for k in (2, 1, 3):
                send(gather.at[own], gather.at[own + 4 - k], *early, {first: wrap(u + k, 4)})
            await_send(gather.at[pl.ds(0, 3)], *early)

            def spread(at, place, count, direction):
                what = gather.at[pl.ds(place, count)]
                return send_one(what, what, *pair(step, at), {second: wrap(w + direction, 4)})

            up, down = spread(1, own, 1, s), spread(2, own, 1, -s)
            yield
            await_recv(gather.at[pl.ds(0, 3)], *early)
            up_rest, down_rest = spread(5, own + 1, 3, s), spread(6, own + 1, 3, -s)
            mine = row(c, w)
            send(mine, mine, *twin, {"c": 1 - c})
            up.wait_recv()
            relay = spread(3, c * 16 + wrap(w - s, 4) * 4, 1, s)
            yield
            up_rest.wait_recv()
            relay_rest = spread(7, c * 16 + wrap(w - s, 4) * 4 + 1, 3, s)
            behind = row(c, wrap(w - s, 4))
            send(behind, behind, *twin, {"c": 1 - c})
            down.wait_recv()
            down_rest.wait_recv()
            ahead = row(c, wrap(w + s, 4))
            send(ahead, ahead, *twin, {"c": 1 - c})
            yield
            relay.wait_recv()
            relay_rest.wait_recv()
            opposite = row(c, wrap(w + 2, 4))
            send(opposite, opposite, *twin, {"c": 1 - c})
            await_send(gather.at[pl.ds(0, 16)], *twin)
            yield
            await_recv(gather.at[pl.ds(0, 16)], *twin)
            products = []
            for slot in range(SLOTS):
                col = cols_ref[slot]
                cx, cy, cc = col // 8, lax.rem(col // 2, 4), lax.rem(col, 2)
                cu, cw = (cx, cy) if x_first else (cy, cx)
                place = cc * 16 + cw * 4 + lax.rem(cu - u + 4, 4)
                products.append(jnp.dot(
                    gather[place], tiles_t[slot], preferred_element_type=jnp.float32
                ))
            for target in range(NZ):
                total = None
                for slot in range(SLOTS):
                    live = jnp.logical_and(rows_ref[slot] == target, slot < count_ref[0])
                    term = products[slot] * jnp.where(live, 1.0, 0.0)
                    total = term if total is None else total + term
                part[ch, target] = total

            arrive = sums_z[step][ch]

            def pass_on(k, value, direction):
                out = rs_send.at[step, ch, k]
                out[...] = value.astype(jnp.bfloat16)
                return send_one(
                    out, arrive.at[k], rs_s.at[step, ch, k], rs_r.at[step, ch, k],
                    {"z": wrap(z + direction, NZ)},
                )

            def mine_for(k):
                return part[ch, wrap(z + k * s, NZ)]

            fore = pass_on(0, mine_for(4), s)
            back = pass_on(4, mine_for(-3), -s)
            yield
            for k in range(1, 4):
                fore.wait_recv()
                fore = pass_on(k, mine_for(4 - k) + arrive[k - 1].astype(jnp.float32), s)
                if k < 3:
                    back.wait_recv()
                    back = pass_on(4 + k, mine_for(k - 3) + arrive[3 + k].astype(jnp.float32), -s)
                yield
            back.wait_recv()
            raw = part[ch, z] + arrive[6].astype(jnp.float32)
            fore.wait_recv()
            raw = raw + arrive[3].astype(jnp.float32)

            g = shared["total"]
            d = damp_row
            if step == 0:
                known["inv"] = lax.rsqrt(g[0:1] + EPS)
                inv = to_col(known["inv"])
                image = raw * inv
                v0 = vec[0, qs, :] * inv
                vec[0, qs, :] = v0
                act[0, qs, :] = image
                dots = [dot(v0, image), dot(image, image), dot(v0, v0)]
            elif step == 1:
                va, aa, vv = g[0:1], g[1:2], g[2:3]
                h00 = va + d * vv
                e = d - h00
                square = aa + 2.0 * e * va + e * e * vv
                h10 = jnp.sqrt(jnp.maximum(square, 0.0) + EPS)
                known.update(vv00=vv)
                store(0, 0, h00, in_chunk)
                store(1, 0, h10, in_chunk)
                e_col, h_col = to_col(e), to_col(1.0 / h10)
                v0, a0 = vec[0, qs, :], act[0, qs, :]
                v1 = (a0 + e_col * v0) * h_col
                image = (raw + e_col * a0) * h_col
                vec[1, qs, :] = v1
                act[1, qs, :] = image
                dots = [dot(v0, image), dot(v1, image), dot(image, image), dot(v0, v1), dot(v1, v1)]
            else:
                va0, va1, aa, v01, v11 = (g[k : k + 1] for k in range(5))
                v00 = known["vv00"]
                h01 = va0 + d * v01
                h11 = va1 + d * v11 - h01 * v01
                e = d - h11
                square = (
                    aa + e * e * v11 + h01 * h01 * v00
                    + 2.0 * e * va1 - 2.0 * h01 * va0 - 2.0 * e * h01 * v01
                )
                h21 = jnp.sqrt(jnp.maximum(square, 0.0) + EPS)
                known.update(v01=v01, v11=v11)
                store(0, 1, h01, in_chunk)
                store(1, 1, h11, in_chunk)
                store(2, 1, h21, in_chunk)
                e_col, f_col, h_col = to_col(e), to_col(h01), to_col(1.0 / h21)
                v0, v1 = vec[0, qs, :], vec[1, qs, :]
                a0, a1 = act[0, qs, :], act[1, qs, :]
                v2 = (a1 + e_col * v1 - f_col * v0) * h_col
                image = (raw + e_col * a1 - f_col * a0) * h_col
                vec[2, qs, :] = v2
                dots = [
                    dot(v0, image), dot(v1, image), dot(v2, image), dot(image, image),
                    dot(v0, v2), dot(v1, v2), dot(v2, v2),
                ]
            if step + 1 < ITERS:
                gathered[step + 1][ch][own] = image.astype(jnp.bfloat16)
            shared["rows"].append(dots)
        yield

        g = shared["total"]
        va0, va1, va2, aa, v02, v12, v22 = (g[k : k + 1] for k in range(7))
        v00, v01, v11 = known["vv00"], known["v01"], known["v11"]
        d = damp_row
        h02 = va0 + d * v02
        h12 = va1 + d * v12 - h02 * v01
        h22 = va2 + d * v22 - h02 * v02 - h12 * v12
        e = d - h22
        square = (
            aa + e * e * v22 + h02 * h02 * v00 + h12 * h12 * v11
            + 2.0 * (e * va2 - h02 * va0 - h12 * va1 - e * h02 * v02 - e * h12 * v12 + h02 * h12 * v01)
        )
        h32 = jnp.sqrt(jnp.maximum(square, 0.0) + EPS)
        store(0, 2, h02, in_chunk)
        store(1, 2, h12, in_chunk)
        store(2, 2, h22, in_chunk)
        store(3, 2, h32, in_chunk)
        e_col, f_col, k_col, h_col = to_col(e), to_col(h02), to_col(h12), to_col(1.0 / h32)
        vec[3, qs, :] = (image + e_col * vec[2, qs, :] - f_col * vec[0, qs, :] - k_col * vec[1, qs, :]) * h_col

    def store(i, j, row, mask):
        hess_v[i, j : j + 1, :] = jnp.where(mask, row, hess_v[i, j : j + 1, :])

    outs = []

    def emit(i):
        for k in range(TILE // 128):
            out_v[i, k * 128 : (k + 1) * 128, :] = vec[i, :, k * 128 : (k + 1) * 128].T * rescale
        copy = pltpu.make_async_copy(out_v.at[i], basis_ref.at[i], out_sem.at[i])
        copy.start()
        outs.append(copy)

    def together(group):
        shared = {"rows": [], "total": None}
        members = [chunk(group * GROUP + k, shared) for k in range(GROUP)]
        for which in range(ITERS + 1):
            for member in members:
                next(member)
            rows = [functools.reduce(jnp.add, same) for same in zip(*shared["rows"])]
            shared["rows"] = []
            summing, result = reduced(which, group, rows)
            next(summing)
            yield
            if which < ITERS:
                for tick in range(1, STEP_TICKS):
                    if tick in SUM_TICKS:
                        next(summing, None)
                    for member in members:
                        next(member)
                    yield
            for _ in summing:
                if which == ITERS:
                    yield
            shared["total"] = result[0]
        for member in members:
            next(member, None)

    groups = CHUNKS // GROUP
    live = {group: together(group) for group in range(groups)}
    ticks = [0] * groups
    tick = 0
    emitted = 0
    while live:
        for group in list(live):
            if tick >= group * STAGGER:
                try:
                    next(live[group])
                    ticks[group] += 1
                except StopIteration:
                    del live[group]
        if tick == 0:
            for _ in setup():
                pass
        tick += 1
        if emitted < ITERS and min(ticks) > STEP_TICKS * (emitted + 1):
            emit(emitted)
            emitted += 1
    while emitted < ITERS + 1:
        emit(emitted)
        emitted += 1
    hess_copy = pltpu.make_async_copy(hess_v, hess_ref, out_sem.at[ITERS + 1])
    hess_copy.start()
    for copy in sent:
        copy.wait_send()
    for copy in outs:
        copy.wait()
    hess_copy.wait()


def on_device(tiles, tile_row, tile_col, tile_count, damping, right_side):
    width, queries = right_side.shape
    rescale = math.sqrt(width * NX * NY * NZ * 2)
    smem = pl.BlockSpec(memory_space=pltpu.SMEM)
    vmem = pl.BlockSpec(memory_space=pltpu.VMEM)
    hbm = pl.BlockSpec(memory_space=pl.ANY)
    dma = pltpu.SemaphoreType.DMA
    bf16, f32 = jnp.bfloat16, jnp.float32
    basis, hessenberg = pl.pallas_call(
        functools.partial(kernel, rescale),
        out_shape=(
            jax.ShapeDtypeStruct((ITERS + 1, width, queries), f32),
            jax.ShapeDtypeStruct((ITERS + 1, ITERS, queries), f32),
        ),
        in_specs=[smem, smem, smem, vmem, hbm, hbm],
        out_specs=(hbm, hbm),
        scratch_shapes=[pltpu.VMEM((PLANE, QC, TILE), bf16) for _ in range(ITERS * CHUNKS)]
        + [pltpu.VMEM((7, QC, TILE), bf16) for _ in range(ITERS * CHUNKS)]
        + [
            pltpu.VMEM((SLOTS, TILE, TILE), bf16),
            pltpu.VMEM((SLOTS, TILE, TILE), bf16),
            pltpu.VMEM((TILE, QUERIES), f32),
            pltpu.VMEM((ITERS + 1, QUERIES, TILE), f32),
            pltpu.VMEM((ITERS, QUERIES, TILE), f32),
            pltpu.VMEM((CHUNKS, NZ, QC, TILE), f32),
            pltpu.VMEM((ITERS, CHUNKS, 7, QC, TILE), bf16),
            pltpu.VMEM((8, QUERIES), f32),
            pltpu.VMEM((ITERS + 1, TILE, QUERIES), f32),
            pltpu.VMEM((ITERS + 1, ITERS, QUERIES), f32),
            pltpu.VMEM((ITERS + 1, CHUNKS // GROUP, NZ * 2, 8, 128), f32),
            pltpu.VMEM((ITERS + 1, CHUNKS // GROUP, NX * NY, 8, 128), f32),
            dma((2,)),
            dma((ITERS + 2,)),
            dma((ITERS, CHUNKS, 8)),
            dma((ITERS, CHUNKS, 8)),
            dma((ITERS, CHUNKS, 7)),
            dma((ITERS, CHUNKS, 7)),
            dma((ITERS + 1, CHUNKS // GROUP, 2)),
            dma((ITERS + 1, CHUNKS // GROUP, 2)),
        ],
        compiler_params=pltpu.CompilerParams(
            collective_id=0, has_side_effects=True, vmem_limit_bytes=60 * 1024 * 1024
        ),
    )(
        tile_row.reshape(SLOTS), tile_col.reshape(SLOTS), tile_count.reshape(1),
        damping.reshape(1, queries), right_side, tiles.reshape(SLOTS, TILE, TILE),
    )
    return basis, hessenberg


def solution(mesh):
    finer = Mesh(mesh.devices.reshape(NZ, NX, NY, 2), ("z", "x", "y", "c"))
    rows = ("x", "y", "c")
    return jax.shard_map(
        on_device,
        mesh=finer,
        in_specs=(
            P(rows, "z", None, None, None),
            P(rows, "z", None),
            P(rows, "z", None),
            P(rows, "z"),
            P(),
            P((*rows, "z"), None),
        ),
        out_specs=(P(None, (*rows, "z"), None), P()),
        check_vma=False,
    )
```

```python
import functools
import math

import jax
import jax.numpy as jnp
from jax import lax
from jax.experimental import pallas as pl
from jax.experimental.pallas import tpu as pltpu
from jax.sharding import Mesh
from jax.sharding import PartitionSpec as P

EPS = 1e-06
ITERS = 3
SLOTS = 4
TILE = 512
QUERIES = 128
CHUNKS = 4
QC = QUERIES // CHUNKS
GROUP = 4
STAGGER = 0
STEP_TICKS = 8
SUM_TICKS = (2, 5)
NX, NY, NZ = 4, 4, 8
PLANE = NX * NY * 2


def wrap(value, count):
    return lax.rem(value + 2 * count, count)


def kernel(
    rescale,
    rows_ref, cols_ref, count_ref, damping_ref, right_ref, tiles_ref,
    basis_ref, hess_ref,
    *scratch,
):
    refs = list(scratch)
    gathered = [[refs.pop(0) for _ in range(CHUNKS)] for _ in range(ITERS)]
    sums_z = [[refs.pop(0) for _ in range(CHUNKS)] for _ in range(ITERS)]
    (tiles_in, tiles_t, right_v, vec, act, part, rs_send, damp_col, out_v, hess_v,
     ar_z, ar_c, ar_xy,
     in_sem, out_sem, ag_s, ag_r, rs_s, rs_r, ar_s, ar_r) = refs

    x, y, z, c = (lax.axis_index(name) for name in ("x", "y", "z", "c"))
    s = 1 - 2 * c

    tiles_copy = pltpu.make_async_copy(tiles_ref, tiles_in, in_sem.at[0])
    tiles_copy.start()
    right_copy = pltpu.make_async_copy(right_ref, right_v, in_sem.at[1])
    right_copy.start()

    barrier = pltpu.get_barrier_semaphore()
    across_z = [{"z": wrap(z + k, NZ)} for k in (4, 3, 5, 2, 6, 1, 7)]
    across_xy = [
        {"x": wrap(x + i, NX), "y": wrap(y + k, NY)}
        for i, k in ((2, 2), (1, 2), (3, 2), (2, 1), (2, 3), (1, 1), (3, 3), (1, 3), (3, 1),
                     (2, 0), (0, 2), (1, 0), (3, 0), (0, 1), (0, 3))
    ]
    peers = across_z + across_xy + [{"c": 1 - c}]
    for peer in peers:
        pl.semaphore_signal(barrier, inc=1, device_id=peer, device_id_type=pl.DeviceIdType.MESH)

    sent = []

    def remote(src, dst, send_sem, recv_sem, peer):
        return pltpu.make_async_remote_copy(
            src_ref=src, dst_ref=dst, send_sem=send_sem, recv_sem=recv_sem,
            device_id=peer, device_id_type=pl.DeviceIdType.MESH,
        )

    def send(*what):
        remote(*what).start()

    def send_one(*what):
        copy = remote(*what)
        copy.start()
        sent.append(copy)
        return copy

    def await_recv(size, send_sem, recv_sem):
        remote(size, size, send_sem, recv_sem, {"c": 1 - c}).wait_recv()

    def await_send(size, send_sem, recv_sem):
        sent.append(remote(size, size, send_sem, recv_sem, {"c": 1 - c}))

    right_copy.wait()
    for k in range(TILE // 128):
        vec[0, :, k * 128 : (k + 1) * 128] = right_v[k * 128 : (k + 1) * 128, :].T
    damp_row = damping_ref[...]
    lane = lax.broadcasted_iota(jnp.int32, (QC, 128), 1)
    sub = lax.broadcasted_iota(jnp.int32, (QC, 128), 0)
    hess_v[...] = jnp.zeros_like(hess_v)
    pl.semaphore_wait(barrier, len(peers))

    def setup():
        tiles_copy.wait()
        for slot in range(SLOTS):
            for k in range(TILE // 128):
                tiles_t[slot, :, k * 128 : (k + 1) * 128] = tiles_in[slot, k * 128 : (k + 1) * 128, :].T
            yield

    def reduced(which, group, rows):
        result = []

        def run():
            pad = [jnp.zeros((8 - len(rows), 128), jnp.float32)] if len(rows) < 8 else []
            total = jnp.concatenate(rows + pad, axis=0)
            stages = ((c, [{"c": 1 - c}], ar_c), (z, across_z, ar_z), (x * NY + y, across_xy, ar_xy))
            for at, (me, others, buf) in enumerate(stages):
                here = buf.at[which, group]
                here[me] = total
                sems = ar_s.at[which, group, at], ar_r.at[which, group, at]
                for peer in others:
                    send(here.at[me], here.at[me], *sems, peer)
                await_send(here.at[pl.ds(0, len(others))], *sems)
                yield
                await_recv(here.at[pl.ds(0, len(others))], *sems)
                total = here[0]
                for k in range(1, len(others) + 1):
                    total = total + here[k]
            result.append(total)

        return run(), result

    def chunk(ch, shared):
        q0 = ch * QC
        qs = slice(q0, q0 + QC)
        eye = lane == sub + q0
        in_chunk = (lax.broadcasted_iota(jnp.int32, (1, 128), 1) // QC) == ch
        x_first = ch % 2 == 0
        first, second = ("x", "y") if x_first else ("y", "x")
        u, w = (x, y) if x_first else (y, x)

        def to_row(col):
            return jnp.sum(jnp.where(eye, col, 0.0), axis=0, keepdims=True)

        def to_col(row):
            return jnp.sum(jnp.where(eye, row, 0.0), axis=1, keepdims=True)

        def dot(a, b):
            return to_row(jnp.sum(a * b, axis=1, keepdims=True))

        gather = gathered[0][ch]
        own = c * 16 + w * 4
        right = vec[0, qs, :]
        gather[own] = right.astype(jnp.bfloat16)
        pending = [(right, right)]
        known = {}

        def row(core, place):
            return gather.at[pl.ds(core * 16 + place * 4, 4)]

        def pair(step, k):
            return ag_s.at[step, ch, k], ag_r.at[step, ch, k]

        for step in range(ITERS):
            gather = gathered[step][ch]
            early, twin = pair(step, 0), pair(step, 4)
            for k in (2, 1, 3):
                send(gather.at[own], gather.at[own + 4 - k], *early, {first: wrap(u + k, 4)})
            await_send(gather.at[pl.ds(0, 3)], *early)

            def spread(at, place, count, direction):
                what = gather.at[pl.ds(place, count)]
                return send_one(what, what, *pair(step, at), {second: wrap(w + direction, 4)})

            up, down = spread(1, own, 1, s), spread(2, own, 1, -s)
            shared["rows"].append([dot(*both) for both in pending])
            yield
            await_recv(gather.at[pl.ds(0, 3)], *early)
            up_rest, down_rest = spread(5, own + 1, 3, s), spread(6, own + 1, 3, -s)
            mine = row(c, w)
            send(mine, mine, *twin, {"c": 1 - c})
            up.wait_recv()
            relay = spread(3, c * 16 + wrap(w - s, 4) * 4, 1, s)
            yield
            up_rest.wait_recv()
            relay_rest = spread(7, c * 16 + wrap(w - s, 4) * 4 + 1, 3, s)
            behind = row(c, wrap(w - s, 4))
            send(behind, behind, *twin, {"c": 1 - c})
            down.wait_recv()
            down_rest.wait_recv()
            ahead = row(c, wrap(w + s, 4))
            send(ahead, ahead, *twin, {"c": 1 - c})
            yield
            relay.wait_recv()
            relay_rest.wait_recv()
            opposite = row(c, wrap(w + 2, 4))
            send(opposite, opposite, *twin, {"c": 1 - c})
            await_send(gather.at[pl.ds(0, 16)], *twin)
            yield
            await_recv(gather.at[pl.ds(0, 16)], *twin)
            products = []
            for slot in range(SLOTS):
                col = cols_ref[slot]
                cx, cy, cc = col // 8, lax.rem(col // 2, 4), lax.rem(col, 2)
                cu, cw = (cx, cy) if x_first else (cy, cx)
                place = cc * 16 + cw * 4 + lax.rem(cu - u + 4, 4)
                products.append(jnp.dot(
                    gather[place], tiles_t[slot], preferred_element_type=jnp.float32
                ))
            def partial_sum(k):
                target = wrap(z + k * s, NZ)
                total = None
                for slot in range(SLOTS):
                    live = jnp.logical_and(rows_ref[slot] == target, slot < count_ref[0])
                    term = products[slot] * jnp.where(live, 1.0, 0.0)
                    total = term if total is None else total + term
                return total

            arrive = sums_z[step][ch]

            def pass_on(k, value, direction):
                out = rs_send.at[step, ch, k]
                out[...] = value.astype(jnp.bfloat16)
                return send_one(
                    out, arrive.at[k], rs_s.at[step, ch, k], rs_r.at[step, ch, k],
                    {"z": wrap(z + direction, NZ)},
                )

            def mine_for(k):
                return part[ch, k % NZ]

            fore = pass_on(0, partial_sum(4), s)
            back = pass_on(4, partial_sum(-3), -s)
            for k in (3, -2, 2, -1, 1, 0):
                part[ch, k % NZ] = partial_sum(k)
            yield
            for k in range(1, 4):
                fore.wait_recv()
                fore = pass_on(k, mine_for(4 - k) + arrive[k - 1].astype(jnp.float32), s)
                if k < 3:
                    back.wait_recv()
                    back = pass_on(4 + k, mine_for(k - 3) + arrive[3 + k].astype(jnp.float32), -s)
                yield
            back.wait_recv()
            raw = part[ch, 0] + arrive[6].astype(jnp.float32)
            fore.wait_recv()
            raw = raw + arrive[3].astype(jnp.float32)

            g = shared["total"]
            d = damp_row
            if step == 0:
                known["inv"] = lax.rsqrt(g[0:1] + EPS)
                inv = to_col(known["inv"])
                image = raw * inv
                v0 = vec[0, qs, :] * inv
                vec[0, qs, :] = v0
                act[0, qs, :] = image
                pending = [(v0, image), (image, image), (v0, v0)]
            elif step == 1:
                va, aa, vv = g[0:1], g[1:2], g[2:3]
                h00 = va + d * vv
                e = d - h00
                square = aa + 2.0 * e * va + e * e * vv
                h10 = jnp.sqrt(jnp.maximum(square, 0.0) + EPS)
                known.update(vv00=vv)
                store(0, 0, h00, in_chunk)
                store(1, 0, h10, in_chunk)
                e_col, h_col = to_col(e), to_col(1.0 / h10)
                v0, a0 = vec[0, qs, :], act[0, qs, :]
                v1 = (a0 + e_col * v0) * h_col
                image = (raw + e_col * a0) * h_col
                vec[1, qs, :] = v1
                act[1, qs, :] = image
                pending = [(v0, image), (v1, image), (image, image), (v0, v1), (v1, v1)]
            else:
                va0, va1, aa, v01, v11 = (g[k : k + 1] for k in range(5))
                v00 = known["vv00"]
                h01 = va0 + d * v01
                h11 = va1 + d * v11 - h01 * v01
                e = d - h11
                square = (
                    aa + e * e * v11 + h01 * h01 * v00
                    + 2.0 * e * va1 - 2.0 * h01 * va0 - 2.0 * e * h01 * v01
                )
                h21 = jnp.sqrt(jnp.maximum(square, 0.0) + EPS)
                known.update(v01=v01, v11=v11)
                store(0, 1, h01, in_chunk)
                store(1, 1, h11, in_chunk)
                store(2, 1, h21, in_chunk)
                e_col, f_col, h_col = to_col(e), to_col(h01), to_col(1.0 / h21)
                v0, v1 = vec[0, qs, :], vec[1, qs, :]
                a0, a1 = act[0, qs, :], act[1, qs, :]
                v2 = (a1 + e_col * v1 - f_col * v0) * h_col
                image = (raw + e_col * a1 - f_col * a0) * h_col
                vec[2, qs, :] = v2
                pending = [
                    (v0, image), (v1, image), (v2, image), (image, image), (v0, v2), (v1, v2), (v2, v2)
                ]
            if step + 1 < ITERS:
                gathered[step + 1][ch][own] = image.astype(jnp.bfloat16)
        shared["rows"].append([dot(*both) for both in pending])
        yield

        g = shared["total"]
        va0, va1, va2, aa, v02, v12, v22 = (g[k : k + 1] for k in range(7))
        v00, v01, v11 = known["vv00"], known["v01"], known["v11"]
        d = damp_row
        h02 = va0 + d * v02
        h12 = va1 + d * v12 - h02 * v01
        h22 = va2 + d * v22 - h02 * v02 - h12 * v12
        e = d - h22
        square = (
            aa + e * e * v22 + h02 * h02 * v00 + h12 * h12 * v11
            + 2.0 * (e * va2 - h02 * va0 - h12 * va1 - e * h02 * v02 - e * h12 * v12 + h02 * h12 * v01)
        )
        h32 = jnp.sqrt(jnp.maximum(square, 0.0) + EPS)
        store(0, 2, h02, in_chunk)
        store(1, 2, h12, in_chunk)
        store(2, 2, h22, in_chunk)
        store(3, 2, h32, in_chunk)
        e_col, f_col, k_col, h_col = to_col(e), to_col(h02), to_col(h12), to_col(1.0 / h32)
        vec[3, qs, :] = (image + e_col * vec[2, qs, :] - f_col * vec[0, qs, :] - k_col * vec[1, qs, :]) * h_col

    def store(i, j, row, mask):
        hess_v[i, j : j + 1, :] = jnp.where(mask, row, hess_v[i, j : j + 1, :])

    outs = []

    def emit(i):
        for k in range(TILE // 128):
            out_v[i, k * 128 : (k + 1) * 128, :] = vec[i, :, k * 128 : (k + 1) * 128].T * rescale
        copy = pltpu.make_async_copy(out_v.at[i], basis_ref.at[i], out_sem.at[i])
        copy.start()
        outs.append(copy)

    def together(group):
        shared = {"rows": [], "total": None}
        members = [chunk(group * GROUP + k, shared) for k in range(GROUP)]
        for which in range(ITERS + 1):
            for member in members:
                next(member)
            rows = [functools.reduce(jnp.add, same) for same in zip(*shared["rows"])]
            shared["rows"] = []
            summing, result = reduced(which, group, rows)
            next(summing)
            yield
            if which < ITERS:
                for tick in range(1, STEP_TICKS):
                    if tick in SUM_TICKS:
                        next(summing, None)
                    for member in members:
                        next(member)
                    yield
            for _ in summing:
                if which == ITERS:
                    yield
            shared["total"] = result[0]
        for member in members:
            next(member, None)

    groups = CHUNKS // GROUP
    live = {group: together(group) for group in range(groups)}
    ticks = [0] * groups
    tick = 0
    emitted = 0
    while live:
        for group in list(live):
            if tick >= group * STAGGER:
                try:
                    next(live[group])
                    ticks[group] += 1
                except StopIteration:
                    del live[group]
        if tick == 0:
            for _ in setup():
                pass
        tick += 1
        if emitted < ITERS and min(ticks) > STEP_TICKS * (emitted + 1):
            emit(emitted)
            emitted += 1
    while emitted < ITERS + 1:
        emit(emitted)
        emitted += 1
    hess_copy = pltpu.make_async_copy(hess_v, hess_ref, out_sem.at[ITERS + 1])
    hess_copy.start()
    for copy in sent:
        copy.wait_send()
    for copy in outs:
        copy.wait()
    hess_copy.wait()


def on_device(tiles, tile_row, tile_col, tile_count, damping, right_side):
    width, queries = right_side.shape
    rescale = math.sqrt(width * NX * NY * NZ * 2)
    smem = pl.BlockSpec(memory_space=pltpu.SMEM)
    vmem = pl.BlockSpec(memory_space=pltpu.VMEM)
    hbm = pl.BlockSpec(memory_space=pl.ANY)
    dma = pltpu.SemaphoreType.DMA
    bf16, f32 = jnp.bfloat16, jnp.float32
    basis, hessenberg = pl.pallas_call(
        functools.partial(kernel, rescale),
        out_shape=(
            jax.ShapeDtypeStruct((ITERS + 1, width, queries), f32),
            jax.ShapeDtypeStruct((ITERS + 1, ITERS, queries), f32),
        ),
        in_specs=[smem, smem, smem, vmem, hbm, hbm],
        out_specs=(hbm, hbm),
        scratch_shapes=[pltpu.VMEM((PLANE, QC, TILE), bf16) for _ in range(ITERS * CHUNKS)]
        + [pltpu.VMEM((7, QC, TILE), bf16) for _ in range(ITERS * CHUNKS)]
        + [
            pltpu.VMEM((SLOTS, TILE, TILE), bf16),
            pltpu.VMEM((SLOTS, TILE, TILE), bf16),
            pltpu.VMEM((TILE, QUERIES), f32),
            pltpu.VMEM((ITERS + 1, QUERIES, TILE), f32),
            pltpu.VMEM((ITERS, QUERIES, TILE), f32),
            pltpu.VMEM((CHUNKS, NZ, QC, TILE), f32),
            pltpu.VMEM((ITERS, CHUNKS, 7, QC, TILE), bf16),
            pltpu.VMEM((8, QUERIES), f32),
            pltpu.VMEM((ITERS + 1, TILE, QUERIES), f32),
            pltpu.VMEM((ITERS + 1, ITERS, QUERIES), f32),
            pltpu.VMEM((ITERS + 1, CHUNKS // GROUP, NZ, 8, 128), f32),
            pltpu.VMEM((ITERS + 1, CHUNKS // GROUP, 2, 8, 128), f32),
            pltpu.VMEM((ITERS + 1, CHUNKS // GROUP, NX * NY, 8, 128), f32),
            dma((2,)),
            dma((ITERS + 2,)),
            dma((ITERS, CHUNKS, 8)),
            dma((ITERS, CHUNKS, 8)),
            dma((ITERS, CHUNKS, 7)),
            dma((ITERS, CHUNKS, 7)),
            dma((ITERS + 1, CHUNKS // GROUP, 3)),
            dma((ITERS + 1, CHUNKS // GROUP, 3)),
        ],
        compiler_params=pltpu.CompilerParams(
            collective_id=0, has_side_effects=True, vmem_limit_bytes=60 * 1024 * 1024
        ),
    )(
        tile_row.reshape(SLOTS), tile_col.reshape(SLOTS), tile_count.reshape(1),
        damping.reshape(1, queries), right_side, tiles.reshape(SLOTS, TILE, TILE),
    )
    return basis, hessenberg


def solution(mesh):
    finer = Mesh(mesh.devices.reshape(NZ, NX, NY, 2), ("z", "x", "y", "c"))
    rows = ("x", "y", "c")
    return jax.shard_map(
        on_device,
        mesh=finer,
        in_specs=(
            P(rows, "z", None, None, None),
            P(rows, "z", None),
            P(rows, "z", None),
            P(rows, "z"),
            P(),
            P((*rows, "z"), None),
        ),
        out_specs=(P(None, (*rows, "z"), None), P()),
        check_vma=False,
    )
```

```python
import functools
import math

import jax
import jax.numpy as jnp
from jax import lax
from jax.experimental import pallas as pl
from jax.experimental.pallas import tpu as pltpu
from jax.sharding import Mesh
from jax.sharding import PartitionSpec as P

EPS = 1e-06
ITERS = 3
SLOTS = 4
TILE = 512
QUERIES = 128
CHUNKS = 4
QC = QUERIES // CHUNKS
GROUP = 4
STAGGER = 0
STEP_TICKS = 8
SUM_TICKS = (2, 5)
NX, NY, NZ = 4, 4, 8
PLANE = NX * NY * 2


def wrap(value, count):
    return lax.rem(value + 2 * count, count)


def kernel(
    rescale,
    rows_ref, cols_ref, count_ref, damping_ref, right_ref, tiles_ref,
    basis_ref, hess_ref,
    *scratch,
):
    refs = list(scratch)
    gathered = [[refs.pop(0) for _ in range(CHUNKS)] for _ in range(ITERS)]
    sums_z = [[refs.pop(0) for _ in range(CHUNKS)] for _ in range(ITERS)]
    (tiles_in, tiles_t, right_v, vec, act, part, rs_send, damp_col, out_v, hess_v,
     ar_z, ar_c, ar_xy,
     in_sem, out_sem, ag_s, ag_r, rs_s, rs_r, ar_s, ar_r) = refs

    x, y, z, c = (lax.axis_index(name) for name in ("x", "y", "z", "c"))
    s = 1 - 2 * c

    tiles_copy = pltpu.make_async_copy(tiles_ref, tiles_in, in_sem.at[0])
    tiles_copy.start()
    right_copy = pltpu.make_async_copy(right_ref, right_v, in_sem.at[1])
    right_copy.start()

    barrier = pltpu.get_barrier_semaphore()
    across_z = [{"z": wrap(z + k, NZ)} for k in (4, 3, 5, 2, 6, 1, 7)]
    across_xy = [
        {"x": wrap(x + i, NX), "y": wrap(y + k, NY)}
        for i, k in ((2, 2), (1, 2), (3, 2), (2, 1), (2, 3), (1, 1), (3, 3), (1, 3), (3, 1),
                     (2, 0), (0, 2), (1, 0), (3, 0), (0, 1), (0, 3))
    ]
    peers = across_z + across_xy + [{"c": 1 - c}]
    for peer in peers:
        pl.semaphore_signal(barrier, inc=1, device_id=peer, device_id_type=pl.DeviceIdType.MESH)

    sent = []

    def remote(src, dst, send_sem, recv_sem, peer):
        return pltpu.make_async_remote_copy(
            src_ref=src, dst_ref=dst, send_sem=send_sem, recv_sem=recv_sem,
            device_id=peer, device_id_type=pl.DeviceIdType.MESH,
        )

    def send(*what):
        remote(*what).start()

    def send_one(*what):
        copy = remote(*what)
        copy.start()
        sent.append(copy)
        return copy

    def await_recv(size, send_sem, recv_sem):
        remote(size, size, send_sem, recv_sem, {"c": 1 - c}).wait_recv()

    def await_send(size, send_sem, recv_sem):
        sent.append(remote(size, size, send_sem, recv_sem, {"c": 1 - c}))

    right_copy.wait()
    for k in range(TILE // 128):
        vec[0, :, k * 128 : (k + 1) * 128] = right_v[k * 128 : (k + 1) * 128, :].T
    damp_row = damping_ref[...]
    lane = lax.broadcasted_iota(jnp.int32, (QC, 128), 1)
    sub = lax.broadcasted_iota(jnp.int32, (QC, 128), 0)
    hess_v[...] = jnp.zeros_like(hess_v)
    pl.semaphore_wait(barrier, len(peers))

    def setup():
        tiles_copy.wait()
        for slot in range(SLOTS):
            for k in range(TILE // 128):
                tiles_t[slot, :, k * 128 : (k + 1) * 128] = tiles_in[slot, k * 128 : (k + 1) * 128, :].T
            yield

    def reduced(which, group, rows):
        result = []

        def run():
            pad = [jnp.zeros((8 - len(rows), 128), jnp.float32)] if len(rows) < 8 else []
            total = jnp.concatenate(rows + pad, axis=0)
            stages = ((c, [{"c": 1 - c}], ar_c), (z, across_z, ar_z), (x * NY + y, across_xy, ar_xy))
            for at, (me, others, buf) in enumerate(stages):
                here = buf.at[which, group]
                here[me] = total
                sems = ar_s.at[which, group, at], ar_r.at[which, group, at]
                for peer in others:
                    send(here.at[me], here.at[me], *sems, peer)
                await_send(here.at[pl.ds(0, len(others))], *sems)
                yield
                await_recv(here.at[pl.ds(0, len(others))], *sems)
                total = here[0]
                for k in range(1, len(others) + 1):
                    total = total + here[k]
            result.append(total)

        return run(), result

    def chunk(ch, shared):
        q0 = ch * QC
        qs = slice(q0, q0 + QC)
        eye = lane == sub + q0
        in_chunk = (lax.broadcasted_iota(jnp.int32, (1, 128), 1) // QC) == ch
        x_first = ch % 2 == 0
        first, second = ("x", "y") if x_first else ("y", "x")
        u, w = (x, y) if x_first else (y, x)

        def to_row(col):
            return jnp.sum(jnp.where(eye, col, 0.0), axis=0, keepdims=True)

        def to_col(row):
            return jnp.sum(jnp.where(eye, row, 0.0), axis=1, keepdims=True)

        def dot(a, b):
            return to_row(jnp.sum(a * b, axis=1, keepdims=True))

        gather = gathered[0][ch]
        own = c * 16 + w * 4
        right = vec[0, qs, :]
        gather[own] = right.astype(jnp.bfloat16)
        pending = [(right, right)]
        known = {}

        def row(core, place):
            return gather.at[pl.ds(core * 16 + place * 4, 4)]

        def pair(step, k):
            return ag_s.at[step, ch, k], ag_r.at[step, ch, k]

        for step in range(ITERS):
            gather = gathered[step][ch]
            early, twin = pair(step, 0), pair(step, 4)
            for k in (2, 1, 3):
                send(gather.at[own], gather.at[own + 4 - k], *early, {first: wrap(u + k, 4)})
            await_send(gather.at[pl.ds(0, 3)], *early)

            def spread(at, place, count, direction):
                what = gather.at[pl.ds(place, count)]
                return send_one(what, what, *pair(step, at), {second: wrap(w + direction, 4)})

            up, down = spread(1, own, 1, s), spread(2, own, 1, -s)
            shared["rows"].append([dot(*both) for both in pending])
            yield
            await_recv(gather.at[pl.ds(0, 3)], *early)
            up_rest, down_rest = spread(5, own + 1, 3, s), spread(6, own + 1, 3, -s)
            mine = row(c, w)
            send(mine, mine, *twin, {"c": 1 - c})
            up.wait_recv()
            relay = spread(3, c * 16 + wrap(w - s, 4) * 4, 1, s)
            yield
            up_rest.wait_recv()
            relay_rest = spread(7, c * 16 + wrap(w - s, 4) * 4 + 1, 3, s)
            behind = row(c, wrap(w - s, 4))
            send(behind, behind, *twin, {"c": 1 - c})
            down.wait_recv()
            down_rest.wait_recv()
            ahead = row(c, wrap(w + s, 4))
            send(ahead, ahead, *twin, {"c": 1 - c})
            yield
            relay.wait_recv()
            relay_rest.wait_recv()
            opposite = row(c, wrap(w + 2, 4))
            send(opposite, opposite, *twin, {"c": 1 - c})
            await_send(gather.at[pl.ds(0, 16)], *twin)
            yield
            await_recv(gather.at[pl.ds(0, 16)], *twin)
            products = []
            for slot in range(SLOTS):
                col = cols_ref[slot]
                cx, cy, cc = col // 8, lax.rem(col // 2, 4), lax.rem(col, 2)
                cu, cw = (cx, cy) if x_first else (cy, cx)
                place = cc * 16 + cw * 4 + lax.rem(cu - u + 4, 4)
                products.append(jnp.dot(
                    gather[place], tiles_t[slot], preferred_element_type=jnp.float32
                ))
            def partial_sum(k):
                target = wrap(z + k * s, NZ)
                total = None
                for slot in range(SLOTS):
                    live = jnp.logical_and(rows_ref[slot] == target, slot < count_ref[0])
                    term = products[slot] * jnp.where(live, 1.0, 0.0)
                    total = term if total is None else total + term
                return total

            arrive = sums_z[step][ch]

            def pass_on(k, value, direction):
                out = rs_send.at[step, ch, k]
                out[...] = value.astype(jnp.bfloat16)
                return send_one(
                    out, arrive.at[k], rs_s.at[step, ch, k], rs_r.at[step, ch, k],
                    {"z": wrap(z + direction, NZ)},
                )

            def mine_for(k):
                return part[ch, k % NZ]

            fore = pass_on(0, partial_sum(4), s)
            back = pass_on(4, partial_sum(-3), -s)
            for k in (3, -2, 2, -1, 1, 0):
                part[ch, k % NZ] = partial_sum(k)
            yield
            for k in range(1, 4):
                fore.wait_recv()
                fore = pass_on(k, mine_for(4 - k) + arrive[k - 1].astype(jnp.float32), s)
                if k < 3:
                    back.wait_recv()
                    back = pass_on(4 + k, mine_for(k - 3) + arrive[3 + k].astype(jnp.float32), -s)
                yield
            back.wait_recv()
            raw = part[ch, 0] + arrive[6].astype(jnp.float32)
            fore.wait_recv()
            raw = raw + arrive[3].astype(jnp.float32)

            g = shared["total"]
            d = damp_row
            if step == 0:
                known["inv"] = lax.rsqrt(g[0:1] + EPS)
                inv = to_col(known["inv"])
                image = raw * inv
                v0 = vec[0, qs, :] * inv
                vec[0, qs, :] = v0
                act[0, qs, :] = image
                pending = [(v0, image), (image, image), (v0, v0)]
            elif step == 1:
                va, aa, vv = g[0:1], g[1:2], g[2:3]
                h00 = va + d * vv
                e = d - h00
                square = aa + 2.0 * e * va + e * e * vv
                h10 = jnp.sqrt(jnp.maximum(square, 0.0) + EPS)
                known.update(vv00=vv)
                store(0, 0, h00, in_chunk)
                store(1, 0, h10, in_chunk)
                e_col, h_col = to_col(e), to_col(1.0 / h10)
                v0, a0 = vec[0, qs, :], act[0, qs, :]
                v1 = (a0 + e_col * v0) * h_col
                image = (raw + e_col * a0) * h_col
                vec[1, qs, :] = v1
                act[1, qs, :] = image
                pending = [(v0, image), (v1, image), (image, image), (v0, v1), (v1, v1)]
            else:
                va0, va1, aa, v01, v11 = (g[k : k + 1] for k in range(5))
                v00 = known["vv00"]
                h01 = va0 + d * v01
                h11 = va1 + d * v11 - h01 * v01
                e = d - h11
                square = (
                    aa + e * e * v11 + h01 * h01 * v00
                    + 2.0 * e * va1 - 2.0 * h01 * va0 - 2.0 * e * h01 * v01
                )
                h21 = jnp.sqrt(jnp.maximum(square, 0.0) + EPS)
                known.update(v01=v01, v11=v11)
                store(0, 1, h01, in_chunk)
                store(1, 1, h11, in_chunk)
                store(2, 1, h21, in_chunk)
                e_col, f_col, h_col = to_col(e), to_col(h01), to_col(1.0 / h21)
                v0, v1 = vec[0, qs, :], vec[1, qs, :]
                a0, a1 = act[0, qs, :], act[1, qs, :]
                v2 = (a1 + e_col * v1 - f_col * v0) * h_col
                image = (raw + e_col * a1 - f_col * a0) * h_col
                vec[2, qs, :] = v2
                pending = [
                    (v0, image), (v1, image), (v2, image), (image, image), (v0, v2), (v1, v2), (v2, v2)
                ]
            if step + 1 < ITERS:
                gathered[step + 1][ch][own] = image.astype(jnp.bfloat16)
        shared["rows"].append([dot(*both) for both in pending])
        yield

        g = shared["total"]
        va0, va1, va2, aa, v02, v12, v22 = (g[k : k + 1] for k in range(7))
        v00, v01, v11 = known["vv00"], known["v01"], known["v11"]
        d = damp_row
        h02 = va0 + d * v02
        h12 = va1 + d * v12 - h02 * v01
        h22 = va2 + d * v22 - h02 * v02 - h12 * v12
        e = d - h22
        square = (
            aa + e * e * v22 + h02 * h02 * v00 + h12 * h12 * v11
            + 2.0 * (e * va2 - h02 * va0 - h12 * va1 - e * h02 * v02 - e * h12 * v12 + h02 * h12 * v01)
        )
        h32 = jnp.sqrt(jnp.maximum(square, 0.0) + EPS)
        store(0, 2, h02, in_chunk)
        store(1, 2, h12, in_chunk)
        store(2, 2, h22, in_chunk)
        store(3, 2, h32, in_chunk)
        e_col, f_col, k_col, h_col = to_col(e), to_col(h02), to_col(h12), to_col(1.0 / h32)
        vec[3, qs, :] = (image + e_col * vec[2, qs, :] - f_col * vec[0, qs, :] - k_col * vec[1, qs, :]) * h_col

    def store(i, j, row, mask):
        hess_v[i, j : j + 1, :] = jnp.where(mask, row, hess_v[i, j : j + 1, :])

    outs = []

    def emit(i):
        for k in range(TILE // 128):
            out_v[i, k * 128 : (k + 1) * 128, :] = vec[i, :, k * 128 : (k + 1) * 128].T * rescale
        copy = pltpu.make_async_copy(out_v.at[i], basis_ref.at[i], out_sem.at[i])
        copy.start()
        outs.append(copy)

    def together(group):
        shared = {"rows": [], "total": None}
        members = [chunk(group * GROUP + k, shared) for k in range(GROUP)]
        for which in range(ITERS + 1):
            for member in members:
                next(member)
            rows = [functools.reduce(jnp.add, same) for same in zip(*shared["rows"])]
            shared["rows"] = []
            summing, result = reduced(which, group, rows)
            next(summing)
            yield
            if which < ITERS:
                for tick in range(1, STEP_TICKS):
                    if tick in SUM_TICKS:
                        next(summing, None)
                    for member in members:
                        next(member)
                    yield
            for _ in summing:
                if which == ITERS:
                    yield
            shared["total"] = result[0]
        for member in members:
            next(member, None)

    groups = CHUNKS // GROUP
    live = {group: together(group) for group in range(groups)}
    ticks = [0] * groups
    tick = 0
    emitted = 0
    while live:
        for group in list(live):
            if tick >= group * STAGGER:
                try:
                    next(live[group])
                    ticks[group] += 1
                except StopIteration:
                    del live[group]
        if tick == 0:
            for _ in setup():
                pass
        tick += 1
        if emitted < ITERS and min(ticks) > STEP_TICKS * (emitted + 1):
            emit(emitted)
            emitted += 1
    while emitted < ITERS + 1:
        emit(emitted)
        emitted += 1
    hess_copy = pltpu.make_async_copy(hess_v, hess_ref, out_sem.at[ITERS + 1])
    hess_copy.start()
    for copy in sent:
        copy.wait_send()
    for copy in outs:
        copy.wait()
    hess_copy.wait()


def on_device(tiles, tile_row, tile_col, tile_count, damping, right_side):
    width, queries = right_side.shape
    rescale = math.sqrt(width * NX * NY * NZ * 2)
    smem = pl.BlockSpec(memory_space=pltpu.SMEM)
    vmem = pl.BlockSpec(memory_space=pltpu.VMEM)
    hbm = pl.BlockSpec(memory_space=pl.ANY)
    dma = pltpu.SemaphoreType.DMA
    bf16, f32 = jnp.bfloat16, jnp.float32
    basis, hessenberg = pl.pallas_call(
        functools.partial(kernel, rescale),
        out_shape=(
            jax.ShapeDtypeStruct((ITERS + 1, width, queries), f32),
            jax.ShapeDtypeStruct((ITERS + 1, 8, queries), f32),
        ),
        in_specs=[smem, smem, smem, vmem, hbm, hbm],
        out_specs=(hbm, hbm),
        scratch_shapes=[pltpu.VMEM((PLANE, QC, TILE), bf16) for _ in range(ITERS * CHUNKS)]
        + [pltpu.VMEM((7, QC, TILE), bf16) for _ in range(ITERS * CHUNKS)]
        + [
            pltpu.VMEM((SLOTS, TILE, TILE), bf16),
            pltpu.VMEM((SLOTS, TILE, TILE), bf16),
            pltpu.VMEM((TILE, QUERIES), f32),
            pltpu.VMEM((ITERS + 1, QUERIES, TILE), f32),
            pltpu.VMEM((ITERS, QUERIES, TILE), f32),
            pltpu.VMEM((CHUNKS, NZ, QC, TILE), f32),
            pltpu.VMEM((ITERS, CHUNKS, 7, QC, TILE), bf16),
            pltpu.VMEM((8, QUERIES), f32),
            pltpu.VMEM((ITERS + 1, TILE, QUERIES), f32),
            pltpu.VMEM((ITERS + 1, 8, QUERIES), f32),
            pltpu.VMEM((ITERS + 1, CHUNKS // GROUP, NZ, 8, 128), f32),
            pltpu.VMEM((ITERS + 1, CHUNKS // GROUP, 2, 8, 128), f32),
            pltpu.VMEM((ITERS + 1, CHUNKS // GROUP, NX * NY, 8, 128), f32),
            dma((2,)),
            dma((ITERS + 2,)),
            dma((ITERS, CHUNKS, 8)),
            dma((ITERS, CHUNKS, 8)),
            dma((ITERS, CHUNKS, 7)),
            dma((ITERS, CHUNKS, 7)),
            dma((ITERS + 1, CHUNKS // GROUP, 3)),
            dma((ITERS + 1, CHUNKS // GROUP, 3)),
        ],
        compiler_params=pltpu.CompilerParams(
            collective_id=0, has_side_effects=True, vmem_limit_bytes=60 * 1024 * 1024
        ),
    )(
        tile_row.reshape(SLOTS), tile_col.reshape(SLOTS), tile_count.reshape(1),
        damping.reshape(1, queries), right_side, tiles.reshape(SLOTS, TILE, TILE),
    )
    return basis, hessenberg[:, :ITERS]


def solution(mesh):
    finer = Mesh(mesh.devices.reshape(NZ, NX, NY, 2), ("z", "x", "y", "c"))
    rows = ("x", "y", "c")
    return jax.shard_map(
        on_device,
        mesh=finer,
        in_specs=(
            P(rows, "z", None, None, None),
            P(rows, "z", None),
            P(rows, "z", None),
            P(rows, "z"),
            P(),
            P((*rows, "z"), None),
        ),
        out_specs=(P(None, (*rows, "z"), None), P()),
        check_vma=False,
    )
```
